32 devices in a mesh: layer: 2 (over x), row: 4 (over z), col: 4 (over y, core).
Axes of the slice: x: 2, y: 2, z: 4, core: 2. Of those that a mesh axis runs over, the one named last changes fastest.
Arguments:
- covariance: float32 [16384, 8192], P(('layer', 'row'), 'col'), parts along dimension 0, may hold values from -2 to 20, as said below
- weight: bfloat16 [16384, 2, 1024], P(('layer', 'col', 'row')), parts along dimension 0, may hold values from -6 to 6
- factor_a: bfloat16 [16384, 2, 256], P(('layer', 'col', 'row')), parts along dimension 0, may hold values from -1.5 to 1.5
- factor_b: bfloat16 [4, 256, 1024], P('layer', ('row', 'col')), parts along dimension 0, may hold values from -1.5 to 1.5
Outputs:
- new_a: float32 [16384, 2, 256], P(('layer', 'col', 'row')), parts along dimension 0
- new_b: float32 [4, 256, 1024], P('layer', ('row', 'col')), parts along dimension 0
The draws below stay inside these ranges and needn't reach their ends.
There are 2 independent parts, one for each index of `layer`. The reference program is written for one: setup_inputs(seed, part) draws one part's arguments, and reference() takes and returns one part's arrays. A program takes and returns all parts, laid end to end along the dimension named above; each array names one. Nothing has to cross between parts.
Inputs may be any that keep to these rules, and one draw needn't show every extreme that they name: covariance is symmetric and positive definite.
All inputs are finite; a program needn't handle non-finite values.
Results may differ from the reference program's by a relative error of at most 0.0012.
Values may be sent and summed in bfloat16 or wider, within the bound.
No kernel may reach another device: no remote copies, remote signals or barrier semaphores. Data moves between devices by JAX's collectives and lax.ppermute only.
A program may use at most 64 MiB of HBM per device.

```python
import math
import jax
import jax.numpy as jnp
from jax import lax

D = 8192
O = 1024
R = 256


def draw_covariance(key, part):
    key_noise = jax.random.fold_in(key, 11)
    key_scale = jax.random.fold_in(key, 23)
    entries = jax.random.normal(key_noise, (D, D), jnp.float32)
    symmetric = (entries + entries.T) * (0.35 / math.sqrt(2.0 * D)) + jnp.eye(D, dtype=jnp.float32)
    upper_log = math.log(2.0)
    scales = jnp.exp(jax.random.uniform(key_scale, (D,), jnp.float32, math.log(0.5), upper_log))
    return scales[:, None] * symmetric * scales[None, :]


def block_levels(own_key, shape, shards, low, high):
    gain = 1.0
    for axis_at, shards_of in shards:
        draws = jax.random.uniform(jax.random.fold_in(jax.random.fold_in(own_key, 6), axis_at), (shards_of,), jnp.float32, low / len(shards), high / len(shards))
        gain = gain * jnp.repeat(jnp.exp(draws), shape[axis_at] // shards_of).reshape((-1,) + (1,) * (len(shape) - 1 - axis_at))
    return gain


def bell_draw(stream_key, extent, deviation, reach, pieces=(), kind=jnp.bfloat16):
    level = block_levels(stream_key, extent, pieces, -0.22, 0.18) if pieces else 1.0
    result = jax.random.normal(stream_key, extent, jnp.float32) * deviation * level
    return jnp.minimum(jnp.maximum(result, -reach), reach).astype(kind)


def setup_inputs(seed: int = 0, part: int = 0) -> dict:
    keys = jax.random.split(jax.random.key(seed), 5)
    part_splits = jax.random.split(jax.random.fold_in(keys[4], part), 5)
    covariance = draw_covariance(jax.random.fold_in(jax.random.fold_in(keys[4], part), 71), part)
    weight = bell_draw(part_splits[1], (D, 2, O), 1.0, 6.0, ((0, 16),))
    factor_a = bell_draw(part_splits[2], (D, 2, R), 0.25, 1.5, ((0, 16),))
    factor_b = bell_draw(part_splits[3], (2, R, O), 0.25, 1.5, ((1, 16),))
    return dict(covariance=covariance, weight=weight, factor_a=factor_a, factor_b=factor_b)


def reference(covariance, weight, factor_a, factor_b):
    highest = lax.Precision.HIGHEST
    right_f = factor_b.astype(jnp.float32)
    left_f = factor_a.astype(jnp.float32)
    diff_one = (weight.astype(jnp.float32) - jnp.einsum("nkr,kro->nko", left_f, right_f, precision=highest)).astype(jnp.bfloat16)
    proj_one = jnp.einsum("nko,kro->nkr", diff_one.astype(jnp.float32), right_f, precision=highest)
    grad_one = jnp.dot(covariance, proj_one.reshape(D, 2 * R), precision=highest, preferred_element_type=jnp.float32)
    new_a = left_f + (4.0 / O) * grad_one.reshape(D, 2, R)
    diff_two = (weight.astype(jnp.float32) - jnp.einsum("nkr,kro->nko", new_a, right_f, precision=highest)).astype(jnp.bfloat16)
    field = jnp.dot(covariance, new_a.reshape(D, 2 * R), precision=highest, preferred_element_type=jnp.float32)
    grad_two = jnp.einsum("nkr,nko->kro", field.reshape(D, 2, R), diff_two.astype(jnp.float32), precision=highest)
    new_b = right_f + (8.0 / D) * grad_two
    return new_a, new_b
```

```python
import jax
import jax.numpy as jnp
from jax import lax
from jax.sharding import PartitionSpec as P

CORES = 2


def encode(x, scale):
    u = x * scale
    return (u * jnp.abs(u) * (u * u)).astype(jnp.bfloat16)


def decode(code, scale):
    v = code.astype(jnp.float32)
    root = jnp.sqrt(jnp.sqrt(jnp.abs(v))) * (1.0 / scale)
    return jnp.where(v < 0, -root, root)


SCALE_P = 2.0**-2
SCALE_G = 2.0**-7
SCALE_A = 2.0**-4
SCALE_F = 2.0**-12


def per_device(covariance, weight, factor_a, factor_b):
    high = lax.Precision.HIGH
    f32, bf16 = jnp.float32, jnp.bfloat16
    side = lax.axis_size("row")
    ys = lax.axis_size("col") // CORES
    row = lax.axis_index("row")
    col = lax.axis_index("col")
    y, core = col // CORES, col % CORES
    n, projections, features = weight.shape
    rank = factor_a.shape[2]
    share = factor_b.shape[1]
    total_rows = n * side * side
    step_a = 4.0 / features
    step_b = 8.0 / total_rows

    def swap_core(x):
        return lax.ppermute(x, "col", [(i, i ^ 1) for i in range(ys * CORES)])

    def shift_y(x, s):
        return lax.ppermute(
            x,
            "col",
            [(i, (i // CORES + s) % ys * CORES + i % CORES) for i in range(ys * CORES)],
        )

    def shift_row(x, s):
        return lax.ppermute(x, "row", [(i, (i + s) % side) for i in range(side)])

    def mirror(x):
        return lax.ppermute(
            x,
            ("row", "col"),
            [(i * side + j, j * side + i) for i in range(side) for j in range(side)],
        )

    def ordered(blocks, me, count):
        run = [blocks[(count - 1 - i) % count] for i in range(count)]
        both = jnp.concatenate([b[None] for b in run + run[:-1]])
        return lax.dynamic_slice_in_dim(both, (count - 1 - me) % count, count, 0)

    def pick(x, i):
        return lax.dynamic_index_in_dim(x, i, 0, keepdims=False)

    def gather_b(b):
        z = ordered([b] + [shift_row(b, s) for s in range(1, side)], row, side)
        zy = ordered([z] + [shift_y(z, s) for s in range(1, ys)], y, ys)
        zyc = ordered([zy, swap_core(zy)], core, CORES)
        return zyc.transpose(2, 1, 0, 3, 4).reshape(rank, features)

    mirrored_a = mirror(factor_a.reshape(n, projections * rank)).astype(f32)
    new_a, new_b = [], []
    for k in range(projections):
        b = gather_b(factor_b[k])
        w = weight[:, k].astype(f32)
        diff_one = (
            w - jnp.dot(factor_a[:, k], b, preferred_element_type=f32)
        ).astype(bf16)
        proj = lax.dot_general(
            diff_one, b, (((1,), (1,)), ((), ())), preferred_element_type=f32
        )
        code = encode(proj, SCALE_P)
        panel = ordered(
            [code] + [shift_row(code, s) for s in range(1, side)], row, side
        )
        panel = decode(panel.reshape(side * n, rank), SCALE_P)
        part = jnp.dot(covariance, panel, precision=high, preferred_element_type=f32)
        part = part.reshape(ys, CORES, n, rank).transpose(1, 0, 2, 3)
        part = pick(part, core) + swap_core(pick(part, 1 - core))
        grad = pick(part, y)
        for s in range(1, ys):
            away = encode(pick(part, (y + s) % ys), SCALE_G)
            grad = grad + decode(shift_y(away, s), SCALE_G)
        grad_code = encode(grad, SCALE_G)
        a_mirrored = mirrored_a[:, k * rank : (k + 1) * rank] + step_a * grad
        a_code = encode(a_mirrored, SCALE_A)
        a_y = ordered([a_code] + [shift_y(a_code, s) for s in range(1, ys)], y, ys)
        a_panel = ordered([a_y, swap_core(a_y)], core, CORES)
        a_panel = a_panel.transpose(1, 0, 2, 3).reshape(side * n, rank)
        a_panel = decode(a_panel, SCALE_A)
        part = lax.dot_general(
            covariance,
            a_panel,
            (((0,), (0,)), ((), ())),
            precision=high,
            preferred_element_type=f32,
        ).reshape(side, n, rank)
        field = pick(part, row)
        for s in range(1, side):
            away = encode(pick(part, (row + s) % side), SCALE_F)
            field = field + decode(shift_row(away, s), SCALE_F)
        own_grad = decode(mirror(grad_code), SCALE_G)
        a_new = factor_a[:, k].astype(f32) + step_a * own_grad
        new_a.append(a_new)
        diff_two = (
            w - jnp.dot(a_new, b.astype(f32), precision=high, preferred_element_type=f32)
        ).astype(bf16)
        value = lax.dot_general(
            field,
            diff_two.astype(f32),
            (((0,), (0,)), ((), ())),
            precision=high,
            preferred_element_type=f32,
        )
        value = value.reshape(side, ys, CORES, share, features).transpose(2, 1, 0, 3, 4)
        value = pick(value, core) + swap_core(pick(value, 1 - core))
        mine = pick(value, y)
        for s in range(1, ys):
            mine = mine + shift_y(pick(value, (y + s) % ys), s)
        total = pick(mine, row)
        for s in range(1, side):
            total = total + shift_row(pick(mine, (row + s) % side), s)
        new_b.append(factor_b[k].astype(f32) + step_b * total)
    return jnp.stack(new_a, 1), jnp.stack(new_b, 0)


def solution(mesh):
    in_specs = (
        P(("layer", "row"), "col"),
        P(("layer", "col", "row"), None, None),
        P(("layer", "col", "row"), None, None),
        P("layer", ("row", "col"), None),
    )
    out_specs = (P(("layer", "col", "row"), None, None), P("layer", ("row", "col"), None))
    return jax.shard_map(
        per_device, mesh=mesh, in_specs=in_specs, out_specs=out_specs, check_vma=False
    )
```

```python
import jax
import jax.numpy as jnp
from jax import lax
from jax.experimental import pallas as pl
from jax.experimental.pallas import tpu as pltpu
from jax.sharding import PartitionSpec as P


CORES = 2
F32, BF16 = jnp.float32, jnp.bfloat16
VMEM_LIMIT = 12 * 2**20

SCALE_P = 2.0**-2
SCALE_G = 2.0**-7
SCALE_A = 2.0**-4
SCALE_F = 2.0**-12
SCALE_V = 2.0**-16


def encode(x, scale):
    u = x * scale
    return (u * jnp.abs(u) * (u * u)).astype(BF16)


def decode(code, scale):
    v = code.astype(F32)
    root = lax.rsqrt(lax.rsqrt(jnp.abs(v))) * (1.0 / scale)
    return jnp.where(v < 0, -root, root)


def halves(x):
    high = x.astype(BF16)
    return high, (x - high.astype(F32)).astype(BF16)


def mm(a, b):
    return jnp.dot(a, b, preferred_element_type=F32)


class Queue:
    def __init__(self, meta):
        self.meta = meta

    def call(self, body, grid, ins, outs, shapes, args, scratch=(), alias=None, flops=0, limit=VMEM_LIMIT):
        moved = sum(a.size * a.dtype.itemsize for a in args)
        moved += sum(s.size * s.dtype.itemsize for s in shapes)
        spec = pltpu.PrefetchScalarGridSpec(
            num_scalar_prefetch=1,
            grid=grid,
            in_specs=ins,
            out_specs=outs,
            scratch_shapes=list(scratch),
        )
        got = pl.pallas_call(
            body,
            out_shape=shapes,
            grid_spec=spec,
            input_output_aliases=alias or {},
            cost_estimate=pl.CostEstimate(flops=flops, bytes_accessed=moved, transcendentals=0),
            compiler_params=pltpu.CompilerParams(
                dimension_semantics=("arbitrary",) * len(grid), vmem_limit_bytes=limit
            ),
        )(self.meta, *args)
        self.meta, *got = lax.optimization_barrier((self.meta, *got))
        return got[0] if len(got) == 1 else got


def shape(dims, dtype):
    return jax.ShapeDtypeStruct(dims, dtype)


def split_cov(queue, cov):
    rows, cols = cov.shape
    tile = min(rows, 256)

    def body(m, c, hi, lo):
        hi[...], lo[...] = halves(c[...])

    spec = pl.BlockSpec((tile, cols), lambda i, m: (i, 0))
    return queue.call(
        body, (rows // tile,), [spec], [spec, spec], [shape(cov.shape, BF16)] * 2, [cov],
        limit=3 * VMEM_LIMIT,
    )


def place_b(queue, own, other, from_row, from_y, core_at):
    ys, side, projections, share, features = own.shape
    rank = ys * side * CORES * share

    def body(m, own, other, out):
        s = pl.program_id(0)
        for t in range(ys):
            place = (m[from_row + s] * ys + m[from_y + t]) * CORES
            for ref, core in ((own, m[core_at]), (other, 1 - m[core_at])):
                at = pl.ds(pl.multiple_of((place + core) * share, share), share)
                for k in range(projections):
                    out[k, at, :] = ref[t, 0, k]

    spec = pl.BlockSpec((ys, 1, projections, share, features), lambda s, m: (0, s, 0, 0, 0))
    return queue.call(
        body,
        (side,),
        [spec, spec],
        [pl.BlockSpec((projections, rank, features), lambda s, m: (0, 0, 0))],
        [shape((projections, rank, features), BF16)],
        [own, other],
    )


def project(queue, w, a, b, k):
    rank, features = b.shape[1:]
    n = w.shape[0]
    tile = min(n, 256)

    def body(m, w, a, b, code):
        diff = (w[...].astype(F32) - mm(a[...], b[0])).astype(BF16)
        proj = lax.dot_general(diff, b[0], (((1,), (1,)), ((), ())), preferred_element_type=F32)
        code[...] = encode(proj, SCALE_P)

    return queue.call(
        body,
        (n // tile,),
        [
            pl.BlockSpec((tile, features), lambda i, m: (i, k)),
            pl.BlockSpec((tile, rank), lambda i, m: (i, k)),
            pl.BlockSpec((1, rank, features), lambda i, m: (k, 0, 0)),
        ],
        [pl.BlockSpec((tile, rank), lambda i, m: (i, 0))],
        [shape((n, rank), BF16)],
        [w, a, b],
        flops=4 * n * rank * features,
    )


def product_one(queue, cov, blocks, acc, row_of, count, add=None, coded=False):
    hi, lo = cov
    n, width = blocks[0][0].shape
    whole = count * n == hi.shape[0]
    terms = len(blocks)
    tall = n
    if whole and count % 2 == 0:
        tall, count = 2 * n, count // 2

    def body(m, *refs):
        refs = list(refs)
        his, los, codes = refs[:terms], refs[terms : 2 * terms], refs[2 * terms : 3 * terms]
        refs = refs[3 * terms :]
        acc_ref = refs.pop(0) if acc is not None else None
        add_ref = refs.pop(0) if add is not None else None
        out, p_hi, p_lo = refs

        @pl.when(pl.program_id(0) == 0)
        def _():
            for t in range(terms):
                p_hi[t], p_lo[t] = halves(decode(codes[t][...], SCALE_P))

        got = None
        for t in range(terms):
            c = his[t][...]
            part = mm(c, p_hi[t]) + mm(c, p_lo[t]) + mm(los[t][...], p_hi[t])
            got = part if got is None else got + part
        if acc is not None:
            got = got + acc_ref[...]
        if add is not None:
            got = got + add_ref[...]
        out[...] = encode(got, SCALE_G) if coded else got

    specs = [
        pl.BlockSpec((tall, n), lambda i, m, at=at: (row_of(i, m), m[at])) for _, at in blocks
    ]
    ins = specs + specs + [pl.BlockSpec((n, width), lambda i, m: (0, 0))] * terms
    args = [hi] * terms + [lo] * terms + [code for code, _ in blocks]
    alias = None
    if acc is not None:
        if whole:
            alias = {1 + len(args): 0}
        ins.append(pl.BlockSpec((tall, width), lambda i, m: (row_of(i, m), 0)))
        args.append(acc)
    if add is not None:
        ins.append(pl.BlockSpec((tall, width), lambda i, m: (i, 0)))
        args.append(add)
    return queue.call(
        body,
        (count,),
        ins,
        [pl.BlockSpec((tall, width), lambda i, m: (i, 0))],
        [shape((count * tall, width), BF16 if coded else F32)],
        args,
        scratch=[pltpu.VMEM((terms, n, width), BF16)] * 2,
        alias=alias,
        flops=6 * terms * count * tall * n * width,
    )


def finish_grad(queue, part, codes, mirrored_a, k, step):
    n, width = part.shape
    tile = min(n, 128)
    count = len(codes)

    def body(m, part, a, *rest):
        grad = part[...]
        for ref in rest[:count]:
            grad = grad + decode(ref[...], SCALE_G)
        grad_code, a_code = rest[count:]
        grad_code[...] = encode(grad, SCALE_G)
        a_new = a[...].astype(F32) + step * grad
        a_code[...] = encode(a_new.T, SCALE_A)

    spec = pl.BlockSpec((tile, width), lambda i, m: (i, 0))
    return queue.call(
        body,
        (n // tile,),
        [spec, pl.BlockSpec((tile, width), lambda i, m: (i, k))] + [spec] * count,
        [spec, pl.BlockSpec((width, tile), lambda i, m: (0, i))],
        [shape((n, width), BF16), shape((width, n), BF16)],
        [part, mirrored_a, *codes],
    )


def product_two(queue, cov, blocks, acc, col_of, count, coded=False):
    hi, lo = cov
    width, n = blocks[0][0].shape
    whole = count * n == hi.shape[1]
    terms = len(blocks)

    def body(m, *refs):
        refs = list(refs)
        his, los, codes = refs[:terms], refs[terms : 2 * terms], refs[2 * terms : 3 * terms]
        refs = refs[3 * terms :]
        acc_ref = refs.pop(0) if acc is not None else None
        out, parts = refs

        @pl.when(pl.program_id(0) == 0)
        def _():
            for t in range(terms):
                parts[t, :width], parts[t, width:] = halves(decode(codes[t][...], SCALE_A))

        got = None
        for t in range(terms):
            c = his[t][...]
            both = mm(parts[t], c)
            part = both[:width] + both[width:] + mm(parts[t, :width], los[t][...])
            got = part if got is None else got + part
        if acc is not None:
            got = got + acc_ref[...]
        out[...] = encode(got, SCALE_F) if coded else got

    specs = [
        pl.BlockSpec((n, n), lambda i, m, row=row: (row(m), col_of(i, m))) for _, row in blocks
    ]
    ins = specs + specs + [pl.BlockSpec((width, n), lambda i, m: (0, 0))] * terms
    args = [hi] * terms + [lo] * terms + [code for code, _ in blocks]
    alias = None
    if acc is not None:
        if whole:
            alias = {1 + len(args): 0}
        ins.append(pl.BlockSpec((width, n), lambda i, m: (0, col_of(i, m))))
        args.append(acc)
    return queue.call(
        body,
        (count,),
        ins,
        [pl.BlockSpec((width, n), lambda i, m: (0, i))],
        [shape((width, count * n), BF16 if coded else F32)],
        args,
        scratch=[pltpu.VMEM((terms, 2 * width, n), BF16)],
        alias=alias,
        flops=6 * terms * count * n * n * width,
    )


def second_diff(queue, grad_code, w, a, b, k, step):
    n, rank = grad_code.shape
    features = b.shape[2]
    tile = min(n, 256)

    def body(m, grad_code, w, a, b, new_a, diff):
        a_new = a[...].astype(F32) + step * decode(grad_code[...], SCALE_G)
        new_a[...] = a_new
        high, low = halves(a_new)
        value = mm(high, b[0]) + mm(low, b[0])
        diff[...] = (w[...].astype(F32) - value).astype(BF16)

    narrow = pl.BlockSpec((tile, rank), lambda i, m: (i, 0))
    return queue.call(
        body,
        (n // tile,),
        [
            narrow,
            pl.BlockSpec((tile, features), lambda i, m: (i, k)),
            pl.BlockSpec((tile, rank), lambda i, m: (i, k)),
            pl.BlockSpec((1, rank, features), lambda i, m: (k, 0, 0)),
        ],
        [narrow, pl.BlockSpec((tile, features), lambda i, m: (i, 0))],
        [shape((n, rank), F32), shape((n, features), BF16)],
        [grad_code, w, a, b],
        flops=4 * n * rank * features,
    )


def second_grad(queue, own, codes, diff):
    rank, n = own.shape
    features = diff.shape[1]
    count = len(codes)
    tile = min(features, 512)

    def body(m, own, diff, *rest):
        out, f_hi, f_lo = rest[count:]

        @pl.when(pl.program_id(0) == 0)
        def _():
            field = own[...]
            for ref in rest[:count]:
                field = field + decode(ref[...], SCALE_F)
            f_hi[...], f_lo[...] = halves(field)

        out[...] = mm(f_hi[...], diff[...]) + mm(f_lo[...], diff[...])

    spec = pl.BlockSpec((rank, n), lambda i, m: (0, 0))
    return queue.call(
        body,
        (features // tile,),
        [spec, pl.BlockSpec((n, tile), lambda i, m: (0, i))] + [spec] * count,
        [pl.BlockSpec((rank, tile), lambda i, m: (0, i))],
        [shape((rank, features), F32)],
        [own, diff, *codes],
        scratch=[pltpu.VMEM((rank, n), BF16)] * 2,
        flops=4 * n * rank * features,
    )


def per_device(covariance, weight, factor_a, factor_b):
    side = lax.axis_size("row")
    ys = lax.axis_size("col") // CORES
    row = lax.axis_index("row")
    col = lax.axis_index("col")
    y, core = col // CORES, col % CORES
    n, projections, features = weight.shape
    rank = factor_a.shape[2]
    width = projections * rank
    share = factor_b.shape[1]
    step_a = 4.0 / features
    step_b = 8.0 / (n * side * side)

    def swap_core(x):
        return lax.ppermute(x, "col", [(i, i ^ 1) for i in range(ys * CORES)])

    def shift_y(x, s):
        pairs = [(i, (i // CORES + s) % ys * CORES + i % CORES) for i in range(ys * CORES)]
        return lax.ppermute(x, "col", pairs)

    def shift_row(x, s):
        return lax.ppermute(x, "row", [(i, (i + s) % side) for i in range(side)])

    def mirror(x):
        pairs = [(i * side + j, j * side + i) for i in range(side) for j in range(side)]
        return lax.ppermute(x, ("row", "col"), pairs)

    def pick(x, i, axis=0):
        return lax.dynamic_index_in_dim(x, i, axis, keepdims=False)

    hops, lanes = jnp.arange(side), jnp.arange(ys)
    meta = jnp.concatenate(
        [(row - hops) % side, (row + hops) % side, (y - lanes) % ys, (y + lanes) % ys, core[None]]
    ).astype(jnp.int32)
    from_row, to_row = 0, side
    from_y, to_y = 2 * side, 2 * side + ys
    core_at = 2 * side + 2 * ys
    here = [core, 1 - core, y, row]
    here += [(y + t) % ys for t in range(1, ys)] + [(row + t) % side for t in range(1, side)]
    here = [i.astype(jnp.uint32) for i in here]
    a = factor_a.reshape(n, width)
    w = weight.reshape(n, projections * features)
    meta, a, w, *here = lax.optimization_barrier((meta, a, w, *here))
    own_core, other_core, own_y, own_row = here[:4]
    next_y, next_row = here[3 : 3 + ys], here[2 + ys :]
    queue = Queue(meta)

    z = jnp.stack([factor_b] + [shift_row(factor_b, s) for s in range(1, side)])
    mirrored_a = mirror(factor_a)
    zy = jnp.stack([z] + [shift_y(z, s) for s in range(1, ys)])
    cov = split_cov(queue, covariance)
    cov = [pltpu.with_memory_space_constraint(x, pltpu.VMEM) for x in cov]
    zyc = swap_core(zy)
    if share % 16 == 0:
        b = place_b(queue, zy, zyc, from_row, from_y, core_at)
    else:
        both = jnp.where(core == 0, jnp.stack([zy, zyc]), jnp.stack([zyc, zy]))
        both = jnp.take(both, (y - lanes) % ys, axis=1)
        both = jnp.take(both, (row - hops) % side, axis=2)
        b = both.transpose(3, 2, 1, 0, 4, 5).reshape(projections, rank, features)

    ks = range(projections)
    panels = []
    for k in ks:
        code = project(queue, w, a, b, k)
        panels.append([code] + [shift_row(code, s) for s in range(1, side)])
    mirrored_a = mirrored_a.reshape(n, width)
    late = 2

    def early_one(k, acc, s):
        return product_one(queue, cov, [(panels[k][s], from_row + s)], acc, lambda i, m: i, side)

    def pieces_one(k, acc):
        blocks = [(panels[k][s], from_row + s) for s in range(side - late, side)]

        def piece(row_of, count, add=None, coded=False):
            return product_one(queue, cov, blocks, acc, row_of, count, add, coded)

        far_other = piece(lambda i, m: m[to_y + 1 + i] * CORES + 1 - m[core_at], ys - 1)
        far_add = swap_core(far_other)
        near_other = piece(lambda i, m: m[to_y] * CORES + 1 - m[core_at], 1)
        near_add = swap_core(near_other)
        far_code = piece(
            lambda i, m: m[to_y + 1 + i] * CORES + m[core_at], ys - 1, add=far_add, coded=True
        )
        far = [shift_y(far_code[(s - 1) * n : s * n], s) for s in range(1, ys)]
        near = piece(lambda i, m: m[to_y] * CORES + m[core_at], 1, add=near_add)
        return near, far

    def start_two(k, near, far):
        grad_code, a_code = finish_grad(queue, near, far, mirrored_a, k, step_a)
        codes = [a_code] + [shift_y(a_code, s) for s in range(1, ys)]
        others = [swap_core(x) for x in codes]
        back = mirror(grad_code)
        blocks = []
        for s in range(ys):
            blocks.append((codes[s], lambda m, s=s: m[from_y + s] * CORES + m[core_at]))
            blocks.append((others[s], lambda m, s=s: m[from_y + s] * CORES + 1 - m[core_at]))
        acc = None
        for block in blocks[:-late]:
            acc = product_two(queue, cov, [block], acc, lambda i, m: i, side)
        return acc, blocks[-late:], back

    def pieces_two(acc, blocks):
        landed = []
        for hop in range(1, side):
            piece = product_two(
                queue, cov, blocks, acc, lambda i, m, hop=hop: m[to_row + hop], 1, coded=True
            )
            landed.append(shift_row(piece, hop))
        kept = product_two(queue, cov, blocks, acc, lambda i, m: m[to_row], 1)
        return kept, landed

    def finish_b(k, value):
        value = value.reshape(side, ys, CORES, share, features)
        value = pick(value, own_core, 2) + swap_core(pick(value, other_core, 2))
        mine = pick(value, own_y, 1)
        for s in range(1, ys):
            away = encode(pick(value, next_y[s], 1), SCALE_V)
            mine = mine + decode(shift_y(away, s), SCALE_V)
        total = pick(mine, own_row, 0)
        for s in range(1, side):
            away = encode(pick(mine, next_row[s], 0), SCALE_V)
            total = total + decode(shift_row(away, s), SCALE_V)
        return factor_b[k].astype(F32) + step_b * total

    accs = [None] * projections
    for k in ks:
        accs[k] = early_one(k, None, 0)
    sums, seconds, fields, diffs, new_a, new_b = ({} for _ in range(6))
    for k in range(projections + 1):
        if k < projections:
            for s in range(1, side - late):
                accs[k] = early_one(k, accs[k], s)
            sums[k] = pieces_one(k, accs[k])
        if k > 0:
            fields[k - 1] = pieces_two(*seconds[k - 1][:2])
        if k > 1:
            value = second_grad(queue, fields[k - 2][0], fields[k - 2][1], diffs[k - 2])
            new_b[k - 2] = finish_b(k - 2, value)
        if k > 0:
            new_a[k - 1], diffs[k - 1] = second_diff(
                queue, seconds[k - 1][2], w, a, b, k - 1, step_a
            )
        if k < projections:
            seconds[k] = start_two(k, *sums[k])
    last = projections - 1
    value = second_grad(queue, fields[last][0], fields[last][1], diffs[last])
    new_b[last] = finish_b(last, value)
    return jnp.stack([new_a[k] for k in ks], 1), jnp.stack([new_b[k] for k in ks], 0)


def solution(mesh):
    in_specs = (
        P(("layer", "row"), "col"),
        P(("layer", "col", "row"), None, None),
        P(("layer", "col", "row"), None, None),
        P("layer", ("row", "col"), None),
    )
    out_specs = (P(("layer", "col", "row"), None, None), P("layer", ("row", "col"), None))

    return jax.shard_map(
        per_device, mesh=mesh, in_specs=in_specs, out_specs=out_specs, check_vma=False
    )
```

```python
import jax
import jax.numpy as jnp
from jax import lax
from jax.experimental import pallas as pl
from jax.experimental.pallas import tpu as pltpu
from jax.sharding import PartitionSpec as P


CORES = 2
F32, BF16 = jnp.float32, jnp.bfloat16
VMEM_LIMIT = 12 * 2**20

SCALE_P = 2.0**-2
SCALE_G = 2.0**-7
SCALE_A = 2.0**-4
SCALE_F = 2.0**-12
SCALE_V = 2.0**-16


def encode(x, scale):
    u = x * scale
    return (u * jnp.abs(u) * (u * u)).astype(BF16)


def decode(code, scale):
    v = code.astype(F32)
    root = lax.rsqrt(lax.rsqrt(jnp.abs(v))) * (1.0 / scale)
    return jnp.where(v < 0, -root, root)


def halves(x):
    high = x.astype(BF16)
    return high, (x - high.astype(F32)).astype(BF16)


def mm(a, b):
    return jnp.dot(a, b, preferred_element_type=F32)


class Queue:
    def __init__(self, meta):
        self.meta = meta

    def call(self, body, grid, ins, outs, shapes, args, scratch=(), alias=None, flops=0, limit=VMEM_LIMIT):
        moved = sum(a.size * a.dtype.itemsize for a in args)
        moved += sum(s.size * s.dtype.itemsize for s in shapes)
        spec = pltpu.PrefetchScalarGridSpec(
            num_scalar_prefetch=1,
            grid=grid,
            in_specs=ins,
            out_specs=outs,
            scratch_shapes=list(scratch),
        )
        got = pl.pallas_call(
            body,
            out_shape=shapes,
            grid_spec=spec,
            input_output_aliases=alias or {},
            cost_estimate=pl.CostEstimate(flops=flops, bytes_accessed=moved, transcendentals=0),
            compiler_params=pltpu.CompilerParams(
                dimension_semantics=("arbitrary",) * len(grid), vmem_limit_bytes=limit
            ),
        )(self.meta, *args)
        self.meta, *got = lax.optimization_barrier((self.meta, *got))
        return got[0] if len(got) == 1 else got


def shape(dims, dtype):
    return jax.ShapeDtypeStruct(dims, dtype)


def split_cov(queue, cov):
    rows, cols = cov.shape
    tile = min(rows, 256)

    def body(m, c, hi, lo):
        hi[...], lo[...] = halves(c[...])

    spec = pl.BlockSpec((tile, cols), lambda i, m: (i, 0))
    return queue.call(
        body, (rows // tile,), [spec], [spec, spec], [shape(cov.shape, BF16)] * 2, [cov],
        limit=3 * VMEM_LIMIT,
    )


def place_b(queue, own, other, from_row, from_y, core_at):
    ys, side, projections, share, features = own.shape
    rank = ys * side * CORES * share

    def body(m, own, other, out):
        s = pl.program_id(0)
        for t in range(ys):
            place = (m[from_row + s] * ys + m[from_y + t]) * CORES
            for ref, core in ((own, m[core_at]), (other, 1 - m[core_at])):
                at = pl.ds(pl.multiple_of((place + core) * share, share), share)
                for k in range(projections):
                    out[k, at, :] = ref[t, 0, k]

    spec = pl.BlockSpec((ys, 1, projections, share, features), lambda s, m: (0, s, 0, 0, 0))
    return queue.call(
        body,
        (side,),
        [spec, spec],
        [pl.BlockSpec((projections, rank, features), lambda s, m: (0, 0, 0))],
        [shape((projections, rank, features), BF16)],
        [own, other],
    )


def project(queue, w, a, b, k):
    rank, features = b.shape[1:]
    n = w.shape[0]
    tile = min(n, 256)

    def body(m, w, a, b, code):
        diff = (w[...].astype(F32) - mm(a[...], b[0])).astype(BF16)
        proj = lax.dot_general(diff, b[0], (((1,), (1,)), ((), ())), preferred_element_type=F32)
        code[...] = encode(proj, SCALE_P)

    return queue.call(
        body,
        (n // tile,),
        [
            pl.BlockSpec((tile, features), lambda i, m: (i, k)),
            pl.BlockSpec((tile, rank), lambda i, m: (i, k)),
            pl.BlockSpec((1, rank, features), lambda i, m: (k, 0, 0)),
        ],
        [pl.BlockSpec((tile, rank), lambda i, m: (i, 0))],
        [shape((n, rank), BF16)],
        [w, a, b],
        flops=4 * n * rank * features,
    )


def product_one(queue, cov, blocks, acc, row_of, count, add=None, coded=False):
    hi, lo = cov
    n, width = blocks[0][0][0].shape
    whole = count * n == hi.shape[0]
    terms = len(blocks)
    tall = n
    if whole and count % 2 == 0:
        tall, count = 2 * n, count // 2

    def body(m, *refs):
        refs = list(refs)
        his, los, refs = refs[:terms], refs[terms : 2 * terms], refs[2 * terms :]
        codes = [[refs.pop(0) for _ in got] for got, _ in blocks]
        acc_ref = refs.pop(0) if acc is not None else None
        add_ref = refs.pop(0) if add is not None else None
        out, p_hi, p_lo = refs

        @pl.when(pl.program_id(0) == 0)
        def _():
            for t in range(terms):
                code = sum(ref[...].astype(F32) for ref in codes[t])
                p_hi[t], p_lo[t] = halves(decode(code, SCALE_P))

        got = None
        for t in range(terms):
            c = his[t][...]
            part = mm(c, p_hi[t]) + mm(c, p_lo[t]) + mm(los[t][...], p_hi[t])
            got = part if got is None else got + part
        if acc is not None:
            got = got + acc_ref[...]
        if add is not None:
            got = got + add_ref[...]
        out[...] = encode(got, SCALE_G) if coded else got

    specs = [
        pl.BlockSpec((tall, n), lambda i, m, at=at: (row_of(i, m), m[at])) for _, at in blocks
    ]
    codes = [code for got, _ in blocks for code in got]
    ins = specs + specs + [pl.BlockSpec((n, width), lambda i, m: (0, 0))] * len(codes)
    args = [hi] * terms + [lo] * terms + codes
    alias = None
    if acc is not None:
        if whole:
            alias = {1 + len(args): 0}
        ins.append(pl.BlockSpec((tall, width), lambda i, m: (row_of(i, m), 0)))
        args.append(acc)
    if add is not None:
        ins.append(pl.BlockSpec((tall, width), lambda i, m: (i, 0)))
        args.append(add)
    return queue.call(
        body,
        (count,),
        ins,
        [pl.BlockSpec((tall, width), lambda i, m: (i, 0))],
        [shape((count * tall, width), BF16 if coded else F32)],
        args,
        scratch=[pltpu.VMEM((terms, n, width), BF16)] * 2,
        alias=alias,
        flops=6 * terms * count * tall * n * width,
    )


def finish_grad(queue, part, codes, mirrored_a, step):
    n, width = part.shape
    tile = min(n, 128)
    count, pieces = len(codes), len(mirrored_a)

    def body(m, part, *rest):
        grad = part[...]
        for ref in rest[:count]:
            grad = grad + decode(ref[...], SCALE_G)
        grad_code, a_code = rest[count + pieces :]
        grad_code[...] = encode(grad, SCALE_G)
        a_new = step * grad
        for ref in rest[count : count + pieces]:
            a_new = a_new + ref[...].astype(F32)
        a_code[...] = encode(a_new.T, SCALE_A)

    spec = pl.BlockSpec((tile, width), lambda i, m: (i, 0))
    return queue.call(
        body,
        (n // tile,),
        [spec] * (1 + count + pieces),
        [spec, pl.BlockSpec((width, tile), lambda i, m: (0, i))],
        [shape((n, width), BF16), shape((width, n), BF16)],
        [part, *codes, *mirrored_a],
    )


def product_two(queue, cov, blocks, acc, col_of, count, coded=False, add=None):
    hi, lo = cov
    width, n = blocks[0][0].shape
    whole = count * n == hi.shape[1]
    terms = len(blocks)

    def body(m, *refs):
        refs = list(refs)
        his, los, codes = refs[:terms], refs[terms : 2 * terms], refs[2 * terms : 3 * terms]
        refs = refs[3 * terms :]
        acc_ref = refs.pop(0) if acc is not None else None
        add_ref = refs.pop(0) if add is not None else None
        out, parts = refs

        @pl.when(pl.program_id(0) == 0)
        def _():
            for t in range(terms):
                parts[t, :width], parts[t, width:] = halves(decode(codes[t][...], SCALE_A))

        got = None
        for t in range(terms):
            c = his[t][...]
            both = mm(parts[t], c)
            part = both[:width] + both[width:] + mm(parts[t, :width], los[t][...])
            got = part if got is None else got + part
        if acc is not None:
            got = got + acc_ref[...]
        if add is not None:
            got = got + decode(add_ref[...], SCALE_F)
        out[...] = encode(got, SCALE_F) if coded else got

    specs = [
        pl.BlockSpec((n, n), lambda i, m, row=row: (row(m), col_of(i, m))) for _, row in blocks
    ]
    ins = specs + specs + [pl.BlockSpec((width, n), lambda i, m: (0, 0))] * terms
    args = [hi] * terms + [lo] * terms + [code for code, _ in blocks]
    alias = None
    if acc is not None:
        if whole:
            alias = {1 + len(args): 0}
        ins.append(pl.BlockSpec((width, n), lambda i, m: (0, col_of(i, m))))
        args.append(acc)
    if add is not None:
        ins.append(pl.BlockSpec((width, n), lambda i, m: (0, i)))
        args.append(add)
    return queue.call(
        body,
        (count,),
        ins,
        [pl.BlockSpec((width, n), lambda i, m: (0, i))],
        [shape((width, count * n), BF16 if coded else F32)],
        args,
        scratch=[pltpu.VMEM((terms, 2 * width, n), BF16)],
        alias=alias,
        flops=6 * terms * count * n * n * width,
    )


def second_diff(queue, grad_codes, w, a, b, k, step):
    n, rank = grad_codes[0].shape
    features = b.shape[2]
    tile = min(n, 256)
    pieces = len(grad_codes)

    def body(m, w, a, b, *rest):
        new_a, diff = rest[pieces:]
        code = rest[0][...].astype(F32)
        for ref in rest[1:pieces]:
            code = code + ref[...].astype(F32)
        a_new = a[...].astype(F32) + step * decode(code, SCALE_G)
        new_a[...] = a_new
        high, low = halves(a_new)
        value = mm(high, b[0]) + mm(low, b[0])
        diff[...] = (w[...].astype(F32) - value).astype(BF16)

    narrow = pl.BlockSpec((tile, rank), lambda i, m: (i, 0))
    return queue.call(
        body,
        (n // tile,),
        [
            pl.BlockSpec((tile, features), lambda i, m: (i, k)),
            pl.BlockSpec((tile, rank), lambda i, m: (i, k)),
            pl.BlockSpec((1, rank, features), lambda i, m: (k, 0, 0)),
        ]
        + [narrow] * pieces,
        [narrow, pl.BlockSpec((tile, features), lambda i, m: (i, 0))],
        [shape((n, rank), F32), shape((n, features), BF16)],
        [w, a, b, *grad_codes],
        flops=4 * n * rank * features,
    )


def second_grad(queue, own, codes, diff):
    rank, n = own.shape
    features = diff.shape[1]
    count = len(codes)
    tile = min(features, 512)

    def body(m, own, diff, *rest):
        out, f_hi, f_lo = rest[count:]

        @pl.when(pl.program_id(0) == 0)
        def _():
            field = own[...]
            for ref in rest[:count]:
                field = field + decode(ref[...], SCALE_F)
            f_hi[...], f_lo[...] = halves(field)

        out[...] = mm(f_hi[...], diff[...]) + mm(f_lo[...], diff[...])

    spec = pl.BlockSpec((rank, n), lambda i, m: (0, 0))
    return queue.call(
        body,
        (features // tile,),
        [spec, pl.BlockSpec((n, tile), lambda i, m: (0, i))] + [spec] * count,
        [pl.BlockSpec((rank, tile), lambda i, m: (0, i))],
        [shape((rank, features), F32)],
        [own, diff, *codes],
        scratch=[pltpu.VMEM((rank, n), BF16)] * 2,
        flops=4 * n * rank * features,
    )


def per_device(covariance, weight, factor_a, factor_b):
    side = lax.axis_size("row")
    ys = lax.axis_size("col") // CORES
    row = lax.axis_index("row")
    col = lax.axis_index("col")
    y, core = col // CORES, col % CORES
    n, projections, features = weight.shape
    rank = factor_a.shape[2]
    width = projections * rank
    share = factor_b.shape[1]
    step_a = 4.0 / features
    step_b = 8.0 / (n * side * side)

    def swap_core(x):
        return lax.ppermute(x, "col", [(i, i ^ 1) for i in range(ys * CORES)])

    def shift_y(x, s):
        pairs = [(i, (i // CORES + s) % ys * CORES + i % CORES) for i in range(ys * CORES)]
        return lax.ppermute(x, "col", pairs)

    def shift_row(x, s):
        return lax.ppermute(x, "row", [(i, i ^ s) for i in range(side)])

    def mirror(x):
        pairs = [(i * side + j, j * side + i) for i in range(side) for j in range(side)]
        return [lax.ppermute(x, ("row", "col"), pairs)]

    def pick(x, i, axis=0):
        return lax.dynamic_index_in_dim(x, i, axis, keepdims=False)

    hops, lanes = jnp.arange(side), jnp.arange(ys)
    meta = jnp.concatenate(
        [row ^ hops, row ^ hops, (y - lanes) % ys, (y + lanes) % ys, core[None]]
    ).astype(jnp.int32)
    from_row, to_row = 0, side
    from_y, to_y = 2 * side, 2 * side + ys
    core_at = 2 * side + 2 * ys
    here = [core, 1 - core, y, row]
    here += [(y + t) % ys for t in range(1, ys)] + [row ^ t for t in range(1, side)]
    here = [i.astype(jnp.uint32) for i in here]
    a = factor_a.reshape(n, width)
    w = weight.reshape(n, projections * features)
    meta, a, w, *here = lax.optimization_barrier((meta, a, w, *here))
    own_core, other_core, own_y, own_row = here[:4]
    next_y, next_row = here[3 : 3 + ys], here[2 + ys :]
    queue = Queue(meta)

    z = jnp.stack([factor_b] + [shift_row(factor_b, s) for s in range(1, side)])
    zy = jnp.stack([z] + [shift_y(z, s) for s in range(1, ys)])
    mirrored_a = [mirror(a[:, k * rank : (k + 1) * rank]) for k in range(projections)]
    zyc = swap_core(zy)
    if share % 16 == 0:
        b = place_b(queue, zy, zyc, from_row, from_y, core_at)
    else:
        both = jnp.where(core == 0, jnp.stack([zy, zyc]), jnp.stack([zyc, zy]))
        both = jnp.take(both, (y - lanes) % ys, axis=1)
        both = jnp.take(both, (row - hops) % side, axis=2)
        b = both.transpose(3, 2, 1, 0, 4, 5).reshape(projections, rank, features)

    ks = range(projections)
    relay = side == 4
    ends_in, ends_out, middle = [(0, 1), (3, 2)], [(1, 0), (2, 3)], [(1, 2), (2, 1)]

    def spread(code):
        got = [[code]] + [[shift_row(code, s)] for s in range(1, side)]
        if relay:
            got[3] = [lax.ppermute(code, "row", middle), lax.ppermute(got[2][0], "row", ends_out)]
        return got

    panels = []
    for k in ks:
        code = project(queue, w, a, b, k)
        panels.append(spread(code))
    cov = split_cov(queue, covariance)
    cov = [pltpu.with_memory_space_constraint(x, pltpu.VMEM) for x in cov]
    late = 2

    def early_one(k, acc, s):
        return product_one(queue, cov, [(panels[k][s], from_row + s)], acc, lambda i, m: i, side)

    def pieces_one(k, acc):
        blocks = [(panels[k][s], from_row + s) for s in range(side - late, side)]

        def piece(row_of, count, add=None, coded=False):
            return product_one(queue, cov, blocks, acc, row_of, count, add, coded)

        far_other = piece(lambda i, m: m[to_y + 1 + i] * CORES + 1 - m[core_at], ys - 1)
        far_add = swap_core(far_other)
        near_other = piece(lambda i, m: m[to_y] * CORES + 1 - m[core_at], 1)
        near_add = swap_core(near_other)
        far_code = piece(
            lambda i, m: m[to_y + 1 + i] * CORES + m[core_at], ys - 1, add=far_add, coded=True
        )
        far = [shift_y(far_code[(s - 1) * n : s * n], s) for s in range(1, ys)]
        near = piece(lambda i, m: m[to_y] * CORES + m[core_at], 1, add=near_add)
        return near, far

    def start_two(k, near, far):
        grad_code, a_code = finish_grad(queue, near, far, mirrored_a[k], step_a)
        codes = [a_code] + [shift_y(a_code, s) for s in range(1, ys)]
        others = [swap_core(x) for x in codes]
        blocks = []
        for s in range(ys):
            blocks.append((codes[s], lambda m, s=s: m[from_y + s] * CORES + m[core_at]))
            blocks.append((others[s], lambda m, s=s: m[from_y + s] * CORES + 1 - m[core_at]))
        return blocks, mirror(grad_code)

    def early_two(blocks):
        acc = None
        for block in blocks[:-late]:
            acc = product_two(queue, cov, [block], acc, lambda i, m: i, side)
        return acc, blocks[-late:]

    def away_two(acc, blocks, between):
        landed, passed = [], None
        for hop in away_order(side):
            piece = product_two(
                queue,
                cov,
                blocks,
                acc,
                lambda i, m, hop=hop: m[to_row + hop],
                1,
                coded=True,
                add=passed if relay and hop == 2 else None,
            )
            if relay and hop == 3:
                passed = lax.ppermute(piece, "row", ends_in)
                landed.append(lax.ppermute(piece, "row", middle))
            else:
                landed.append(shift_row(piece, hop))
            if between is not None:
                between()
                between = None
        return landed

    def kept_two(acc, blocks):
        return product_two(queue, cov, blocks, acc, lambda i, m: m[to_row], 1)

    def finish_b(value):
        value = value.reshape(side, ys, CORES, share, features)
        value = pick(value, own_core, 2) + swap_core(pick(value, other_core, 2))
        mine = pick(value, own_y, 1)
        for s in range(1, ys):
            away = encode(pick(value, next_y[s], 1), SCALE_V)
            mine = mine + decode(shift_y(away, s), SCALE_V)
        return mine

    def sum_rows(mine):
        total = pick(mine, own_row, 1)
        for s in range(1, side):
            away = encode(pick(mine, next_row[s], 1), SCALE_V)
            total = total + decode(shift_row(away, s), SCALE_V)
        return factor_b.astype(F32) + step_b * total

    accs = [early_one(k, None, 0) for k in ks]
    sums, seconds, fields, values = [], [], [], []

    new_a, diffs = [], []

    def finish_one(k):
        blocks, back = start_two(k, *sums[k])
        seconds.append([blocks, back])

    def diff_two(k):
        a_new, diff = second_diff(queue, seconds[k][1], w, a, b, k, step_a)
        new_a.append(a_new)
        diffs.append(diff)

    def grad_two(k):
        values.append(finish_b(second_grad(queue, kept[k], fields[k], diffs[k])))

    last = projections - 1
    for k in ks:
        for s in range(1, side - late):
            accs[k] = early_one(k, accs[k], s)
        if k > 0:
            finish_one(k - 1)
            seconds[k - 1][0] = early_two(seconds[k - 1][0])
        sums.append(pieces_one(k, accs[k]))
        if k > 0:
            after = (lambda: finish_one(last)) if k == last else None
            fields.append(away_two(*seconds[k - 1][0], after))
    if last == 0:
        finish_one(last)
    seconds[last][0] = early_two(seconds[last][0])
    fields.append(away_two(*seconds[last][0], None))
    kept = [kept_two(*seconds[k][0]) for k in reversed(ks)][::-1]
    for k in range(last):
        diff_two(k)
        grad_two(k)
    diff_two(last)
    new_a = jnp.stack(new_a, 1)
    queue.meta, new_a = lax.optimization_barrier((queue.meta, new_a))
    grad_two(last)
    return new_a, sum_rows(jnp.stack(values, 0))


def away_order(side):
    return (3, 1, 2) if side == 4 else tuple(range(1, side))


def solution(mesh):
    in_specs = (
        P(("layer", "row"), "col"),
        P(("layer", "col", "row"), None, None),
        P(("layer", "col", "row"), None, None),
        P("layer", ("row", "col"), None),
    )
    out_specs = (P(("layer", "col", "row"), None, None), P("layer", ("row", "col"), None))

    return jax.shard_map(
        per_device, mesh=mesh, in_specs=in_specs, out_specs=out_specs, check_vma=False
    )
```

```python
import jax
import jax.numpy as jnp
from jax import lax
from jax.experimental import pallas as pl
from jax.experimental.pallas import tpu as pltpu
from jax.sharding import PartitionSpec as P


CORES = 2
F32, BF16 = jnp.float32, jnp.bfloat16
VMEM_LIMIT = 12 * 2**20

SCALE_P = 2.0**-2
SCALE_G = 2.0**-7
SCALE_A = 2.0**-4
SCALE_F = 2.0**-12
SCALE_V = 2.0**-16


def encode(x, scale):
    u = x * scale
    return (u * jnp.abs(u) * (u * u)).astype(BF16)


def decode(code, scale):
    v = code.astype(F32)
    root = lax.rsqrt(lax.rsqrt(jnp.abs(v))) * (1.0 / scale)
    return jnp.where(v < 0, -root, root)


def halves(x):
    high = x.astype(BF16)
    return high, (x - high.astype(F32)).astype(BF16)


def mm(a, b):
    return jnp.dot(a, b, preferred_element_type=F32)


class Queue:
    def __init__(self, meta):
        self.meta = meta

    def call(self, body, grid, ins, outs, shapes, args, scratch=(), alias=None, flops=0, limit=VMEM_LIMIT):
        moved = sum(a.size * a.dtype.itemsize for a in args)
        moved += sum(s.size * s.dtype.itemsize for s in shapes)
        spec = pltpu.PrefetchScalarGridSpec(
            num_scalar_prefetch=1,
            grid=grid,
            in_specs=ins,
            out_specs=outs,
            scratch_shapes=list(scratch),
        )
        got = pl.pallas_call(
            body,
            out_shape=shapes,
            grid_spec=spec,
            input_output_aliases=alias or {},
            cost_estimate=pl.CostEstimate(flops=flops, bytes_accessed=moved, transcendentals=0),
            compiler_params=pltpu.CompilerParams(
                dimension_semantics=("arbitrary",) * len(grid), vmem_limit_bytes=limit
            ),
        )(self.meta, *args)
        self.meta, *got = lax.optimization_barrier((self.meta, *got))
        return got[0] if len(got) == 1 else got


def shape(dims, dtype):
    return jax.ShapeDtypeStruct(dims, dtype)


def split_cov(queue, cov):
    rows, cols = cov.shape
    tile = min(rows, 256)

    def body(m, c, hi, lo):
        hi[...], lo[...] = halves(c[...])

    spec = pl.BlockSpec((tile, cols), lambda i, m: (i, 0))
    return queue.call(
        body, (rows // tile,), [spec], [spec, spec], [shape(cov.shape, BF16)] * 2, [cov],
    )


def place_b(queue, own, other, from_row, from_y, core_at):
    ys, side, projections, share, features = own.shape
    rank = ys * side * CORES * share

    def body(m, own, other, out):
        s = pl.program_id(0)
        for t in range(ys):
            place = (m[from_row + s] * ys + m[from_y + t]) * CORES
            for ref, core in ((own, m[core_at]), (other, 1 - m[core_at])):
                at = pl.ds(pl.multiple_of((place + core) * share, share), share)
                for k in range(projections):
                    out[k, at, :] = ref[t, 0, k]

    spec = pl.BlockSpec((ys, 1, projections, share, features), lambda s, m: (0, s, 0, 0, 0))
    return queue.call(
        body,
        (side,),
        [spec, spec],
        [pl.BlockSpec((projections, rank, features), lambda s, m: (0, 0, 0))],
        [shape((projections, rank, features), BF16)],
        [own, other],
    )


def project(queue, w, a, b, k):
    rank, features = b.shape[1:]
    n = w.shape[0]
    tile = min(n, 256)

    def body(m, w, a, b, code):
        diff = (w[...].astype(F32) - mm(a[...], b[0])).astype(BF16)
        proj = lax.dot_general(diff, b[0], (((1,), (1,)), ((), ())), preferred_element_type=F32)
        code[...] = encode(proj, SCALE_P)

    return queue.call(
        body,
        (n // tile,),
        [
            pl.BlockSpec((tile, features), lambda i, m: (i, k)),
            pl.BlockSpec((tile, rank), lambda i, m: (i, k)),
            pl.BlockSpec((1, rank, features), lambda i, m: (k, 0, 0)),
        ],
        [pl.BlockSpec((tile, rank), lambda i, m: (i, 0))],
        [shape((n, rank), BF16)],
        [w, a, b],
        flops=4 * n * rank * features,
    )


def product_one(queue, cov, blocks, acc, row_of, count, add=None, coded=False, ready=None, emit=False):
    hi, lo = cov
    n, width = blocks[0][0][0].shape
    fresh = ready is None
    whole = count * n == hi.shape[0]
    terms = len(blocks)
    tall = n
    if whole and count % 2 == 0:
        tall, count = 2 * n, count // 2

    def body(m, *refs):
        refs = list(refs)
        his, los, refs = refs[:terms], refs[terms : 2 * terms], refs[2 * terms :]
        if fresh:
            codes = [[refs.pop(0) for _ in got] for got, _ in blocks]
        else:
            p_hi, p_lo = refs.pop(0), refs.pop(0)
        acc_ref = refs.pop(0) if acc is not None else None
        add_ref = refs.pop(0) if add is not None else None
        out = refs.pop(0)
        if fresh:
            p_hi, p_lo = refs

        @pl.when(fresh and pl.program_id(0) == 0)
        def _():
            for t in range(terms):
                code = sum(ref[...].astype(F32) for ref in codes[t])
                p_hi[t], p_lo[t] = halves(decode(code, SCALE_P))

        got = None
        for t in range(terms):
            c = his[t][...]
            part = mm(c, p_hi[t]) + mm(c, p_lo[t]) + mm(los[t][...], p_hi[t])
            got = part if got is None else got + part
        if acc is not None:
            got = got + acc_ref[...]
        if add is not None:
            got = got + add_ref[...]
        out[...] = encode(got, SCALE_G) if coded else got

    specs = [
        pl.BlockSpec((tall, n), lambda i, m, at=at: (row_of(i, m), m[at])) for _, at in blocks
    ]
    codes = [code for got, _ in blocks for code in got] if fresh else list(ready)
    parts = pl.BlockSpec((terms, n, width), lambda i, m: (0, 0, 0))
    held = pl.BlockSpec((n, width), lambda i, m: (0, 0)) if fresh else parts
    ins = specs + specs + [held] * len(codes)
    args = [hi] * terms + [lo] * terms + codes
    alias = None
    if acc is not None:
        if whole:
            alias = {1 + len(args): 0}
        ins.append(pl.BlockSpec((tall, width), lambda i, m: (row_of(i, m), 0)))
        args.append(acc)
    if add is not None:
        ins.append(pl.BlockSpec((tall, width), lambda i, m: (i, 0)))
        args.append(add)
    return queue.call(
        body,
        (count,),
        ins,
        [pl.BlockSpec((tall, width), lambda i, m: (i, 0))] + [parts] * (2 * emit),
        [shape((count * tall, width), BF16 if coded else F32)]
        + [shape((terms, n, width), BF16)] * (2 * emit),
        args,
        scratch=[pltpu.VMEM((terms, n, width), BF16)] * (2 * (fresh and not emit)),
        alias=alias,
        flops=6 * terms * count * tall * n * width,
    )


def finish_grad(queue, part, codes, mirrored_a, step):
    n, width = part.shape
    tile = min(n, 128)
    count, pieces = len(codes), len(mirrored_a)

    def body(m, part, *rest):
        grad = part[...]
        for ref in rest[:count]:
            grad = grad + decode(ref[...], SCALE_G)
        grad_code, a_code = rest[count + pieces :]
        grad_code[...] = encode(grad, SCALE_G)
        a_new = step * grad
        for ref in rest[count : count + pieces]:
            a_new = a_new + ref[...].astype(F32)
        a_code[...] = encode(a_new.T, SCALE_A)

    spec = pl.BlockSpec((tile, width), lambda i, m: (i, 0))
    return queue.call(
        body,
        (n // tile,),
        [spec] * (1 + count + pieces),
        [spec, pl.BlockSpec((width, tile), lambda i, m: (0, i))],
        [shape((n, width), BF16), shape((width, n), BF16)],
        [part, *codes, *mirrored_a],
    )


def product_two(queue, cov, blocks, acc, col_of, count, coded=False, add=None, ready=None, emit=False):
    hi, lo = cov
    width, n = blocks[0][0].shape
    fresh = ready is None
    whole = count * n == hi.shape[1]
    terms = len(blocks)

    def body(m, *refs):
        refs = list(refs)
        his, los, refs = refs[:terms], refs[terms : 2 * terms], refs[2 * terms :]
        codes = [refs.pop(0) for _ in blocks] if fresh else []
        parts = None if fresh else refs.pop(0)
        acc_ref = refs.pop(0) if acc is not None else None
        add_ref = refs.pop(0) if add is not None else None
        out = refs.pop(0)
        if fresh:
            (parts,) = refs

        @pl.when(fresh and pl.program_id(0) == 0)
        def _():
            for t in range(terms):
                parts[t, :width], parts[t, width:] = halves(decode(codes[t][...], SCALE_A))

        got = None
        for t in range(terms):
            c = his[t][...]
            both = mm(parts[t], c)
            part = both[:width] + both[width:] + mm(parts[t, :width], los[t][...])
            got = part if got is None else got + part
        if acc is not None:
            got = got + acc_ref[...]
        if add is not None:
            got = got + decode(add_ref[...], SCALE_F)
        out[...] = encode(got, SCALE_F) if coded else got

    specs = [
        pl.BlockSpec((n, n), lambda i, m, row=row: (row(m), col_of(i, m))) for _, row in blocks
    ]
    whole_parts = pl.BlockSpec((terms, 2 * width, n), lambda i, m: (0, 0, 0))
    codes = [code for code, _ in blocks] if fresh else [ready]
    held = pl.BlockSpec((width, n), lambda i, m: (0, 0)) if fresh else whole_parts
    ins = specs + specs + [held] * len(codes)
    args = [hi] * terms + [lo] * terms + codes
    alias = None
    if acc is not None:
        if whole:
            alias = {1 + len(args): 0}
        ins.append(pl.BlockSpec((width, n), lambda i, m: (0, col_of(i, m))))
        args.append(acc)
    if add is not None:
        ins.append(pl.BlockSpec((width, n), lambda i, m: (0, i)))
        args.append(add)
    return queue.call(
        body,
        (count,),
        ins,
        [pl.BlockSpec((width, n), lambda i, m: (0, i))] + [whole_parts] * emit,
        [shape((width, count * n), BF16 if coded else F32)]
        + [shape((terms, 2 * width, n), BF16)] * emit,
        args,
        scratch=[pltpu.VMEM((terms, 2 * width, n), BF16)] * (fresh and not emit),
        alias=alias,
        flops=6 * terms * count * n * n * width,
    )


def second_diff(queue, grad_codes, w, a, b, k, step):
    n, rank = grad_codes[0].shape
    features = b.shape[2]
    tile = min(n, 256)
    pieces = len(grad_codes)

    def body(m, w, a, b, *rest):
        new_a, diff = rest[pieces:]
        code = rest[0][...].astype(F32)
        for ref in rest[1:pieces]:
            code = code + ref[...].astype(F32)
        a_new = a[...].astype(F32) + step * decode(code, SCALE_G)
        new_a[...] = a_new
        high, low = halves(a_new)
        value = mm(high, b[0]) + mm(low, b[0])
        diff[...] = (w[...].astype(F32) - value).astype(BF16)

    narrow = pl.BlockSpec((tile, rank), lambda i, m: (i, 0))
    return queue.call(
        body,
        (n // tile,),
        [
            pl.BlockSpec((tile, features), lambda i, m: (i, k)),
            pl.BlockSpec((tile, rank), lambda i, m: (i, k)),
            pl.BlockSpec((1, rank, features), lambda i, m: (k, 0, 0)),
        ]
        + [narrow] * pieces,
        [narrow, pl.BlockSpec((tile, features), lambda i, m: (i, 0))],
        [shape((n, rank), F32), shape((n, features), BF16)],
        [w, a, b, *grad_codes],
        flops=4 * n * rank * features,
    )


def second_grad(queue, own, codes, diff):
    rank, n = own.shape
    features = diff.shape[1]
    count = len(codes)
    tile = min(features, 512)

    def body(m, own, diff, *rest):
        out, f_hi, f_lo = rest[count:]

        @pl.when(pl.program_id(0) == 0)
        def _():
            field = own[...]
            for ref in rest[:count]:
                field = field + decode(ref[...], SCALE_F)
            f_hi[...], f_lo[...] = halves(field)

        out[...] = mm(f_hi[...], diff[...]) + mm(f_lo[...], diff[...])

    spec = pl.BlockSpec((rank, n), lambda i, m: (0, 0))
    return queue.call(
        body,
        (features // tile,),
        [spec, pl.BlockSpec((n, tile), lambda i, m: (0, i))] + [spec] * count,
        [pl.BlockSpec((rank, tile), lambda i, m: (0, i))],
        [shape((rank, features), F32)],
        [own, diff, *codes],
        scratch=[pltpu.VMEM((rank, n), BF16)] * 2,
        flops=4 * n * rank * features,
    )


def per_device(covariance, weight, factor_a, factor_b):
    side = lax.axis_size("row")
    ys = lax.axis_size("col") // CORES
    row = lax.axis_index("row")
    col = lax.axis_index("col")
    y, core = col // CORES, col % CORES
    n, projections, features = weight.shape
    rank = factor_a.shape[2]
    width = projections * rank
    share = factor_b.shape[1]
    step_a = 4.0 / features
    step_b = 8.0 / (n * side * side)

    def swap_core(x):
        return lax.ppermute(x, "col", [(i, i ^ 1) for i in range(ys * CORES)])

    def shift_y(x, s):
        pairs = [(i, (i // CORES + s) % ys * CORES + i % CORES) for i in range(ys * CORES)]
        return lax.ppermute(x, "col", pairs)

    def shift_row(x, s):
        return lax.ppermute(x, "row", [(i, i ^ s) for i in range(side)])

    def mirror(x):
        pairs = [(i * side + j, j * side + i) for i in range(side) for j in range(side)]
        return [lax.ppermute(x, ("row", "col"), pairs)]

    def pick(x, i, axis=0):
        return lax.dynamic_index_in_dim(x, i, axis, keepdims=False)

    hops, lanes = jnp.arange(side), jnp.arange(ys)
    meta = jnp.concatenate(
        [row ^ hops, row ^ hops, (y - lanes) % ys, (y + lanes) % ys, core[None]]
    ).astype(jnp.int32)
    from_row, to_row = 0, side
    from_y, to_y = 2 * side, 2 * side + ys
    core_at = 2 * side + 2 * ys
    here = [core, 1 - core, y, row]
    here += [(y + t) % ys for t in range(1, ys)] + [row ^ t for t in range(1, side)]
    here = [i.astype(jnp.uint32) for i in here]
    a = factor_a.reshape(n, width)
    w = weight.reshape(n, projections * features)
    meta, a, w, *here = lax.optimization_barrier((meta, a, w, *here))
    own_core, other_core, own_y, own_row = here[:4]
    next_y, next_row = here[3 : 3 + ys], here[2 + ys :]
    queue = Queue(meta)

    z = jnp.stack([factor_b] + [shift_row(factor_b, s) for s in range(1, side)])
    zy = jnp.stack([z] + [shift_y(z, s) for s in range(1, ys)])
    mirrored_a = [mirror(a[:, k * rank : (k + 1) * rank]) for k in range(projections)]
    zyc = swap_core(zy)
    if share % 16 == 0:
        b = place_b(queue, zy, zyc, from_row, from_y, core_at)
    else:
        both = jnp.where(core == 0, jnp.stack([zy, zyc]), jnp.stack([zyc, zy]))
        both = jnp.take(both, (y - lanes) % ys, axis=1)
        both = jnp.take(both, (row - hops) % side, axis=2)
        b = both.transpose(3, 2, 1, 0, 4, 5).reshape(projections, rank, features)

    ks = range(projections)
    relay = side == 4
    ends_in, ends_out, middle = [(0, 1), (3, 2)], [(1, 0), (2, 3)], [(1, 2), (2, 1)]

    def spread(code):
        got = [[code]] + [[shift_row(code, s)] for s in range(1, side)]
        if relay:
            got[3] = [lax.ppermute(code, "row", middle), lax.ppermute(got[2][0], "row", ends_out)]
        return got

    panels = []
    for k in ks:
        code = project(queue, w, a, b, k)
        panels.append(spread(code))
    cov = split_cov(queue, covariance)
    cov = [pltpu.with_memory_space_constraint(x, pltpu.VMEM) for x in cov]
    late = 2

    def early_one(k, acc, s):
        return product_one(queue, cov, [(panels[k][s], from_row + s)], acc, lambda i, m: i, side)

    def pieces_one(k, acc):
        blocks = [(panels[k][s], from_row + s) for s in range(side - late, side)]

        ready = None

        def piece(row_of, count, add=None, coded=False):
            first = ready is None
            return product_one(queue, cov, blocks, acc, row_of, count, add, coded, ready, first)

        far_other, *ready = piece(lambda i, m: m[to_y + 1 + i] * CORES + 1 - m[core_at], ys - 1)
        far_add = swap_core(far_other)
        near_other = piece(lambda i, m: m[to_y] * CORES + 1 - m[core_at], 1)
        near_add = swap_core(near_other)
        far_code = piece(
            lambda i, m: m[to_y + 1 + i] * CORES + m[core_at], ys - 1, add=far_add, coded=True
        )
        far = [shift_y(far_code[(s - 1) * n : s * n], s) for s in range(1, ys)]
        near = piece(lambda i, m: m[to_y] * CORES + m[core_at], 1, add=near_add)
        return near, far

    def start_two(k, near, far):
        grad_code, a_code = finish_grad(queue, near, far, mirrored_a[k], step_a)
        codes = [a_code] + [shift_y(a_code, s) for s in range(1, ys)]
        others = [swap_core(x) for x in codes]
        blocks = []
        for s in range(ys):
            blocks.append((codes[s], lambda m, s=s: m[from_y + s] * CORES + m[core_at]))
            blocks.append((others[s], lambda m, s=s: m[from_y + s] * CORES + 1 - m[core_at]))
        return blocks, mirror(grad_code)

    def early_two(blocks):
        acc = None
        for block in blocks[:-late]:
            acc = product_two(queue, cov, [block], acc, lambda i, m: i, side)
        return acc, blocks[-late:]

    def away_two(k, acc, blocks, between):
        landed, passed, ready = [], None, None
        for hop in away_order(side):
            piece = product_two(
                queue,
                cov,
                blocks,
                acc,
                lambda i, m, hop=hop: m[to_row + hop],
                1,
                coded=True,
                add=passed if relay and hop == 2 else None,
                ready=ready,
                emit=ready is None,
            )
            if ready is None:
                piece, ready = piece
            parts_two[k] = ready
            if relay and hop == 3:
                passed = lax.ppermute(piece, "row", ends_in)
                landed.append(lax.ppermute(piece, "row", middle))
            else:
                landed.append(shift_row(piece, hop))
            if between is not None:
                between()
                between = None
        return landed

    def kept_two(k, acc, blocks):
        return product_two(
            queue, cov, blocks, acc, lambda i, m: m[to_row], 1,
            ready=parts_two[k],
        )

    def finish_b(value):
        value = value.reshape(side, ys, CORES, share, features)
        value = pick(value, own_core, 2) + swap_core(pick(value, other_core, 2))
        mine = pick(value, own_y, 1)
        for s in range(1, ys):
            away = encode(pick(value, next_y[s], 1), SCALE_V)
            mine = mine + decode(shift_y(away, s), SCALE_V)
        return mine

    def sum_rows(mine):
        total = pick(mine, own_row, 1)
        for s in range(1, side):
            away = encode(pick(mine, next_row[s], 1), SCALE_V)
            total = total + decode(shift_row(away, s), SCALE_V)
        return factor_b.astype(F32) + step_b * total

    accs = [early_one(k, None, 0) for k in ks]
    sums, seconds, fields, values = [], [], [], []

    new_a, diffs, parts_two = [], [], {}

    def finish_one(k):
        blocks, back = start_two(k, *sums[k])
        seconds.append([blocks, back])

    def diff_two(k):
        a_new, diff = second_diff(queue, seconds[k][1], w, a, b, k, step_a)
        new_a.append(a_new)
        diffs.append(diff)

    def grad_two(k):
        values.append(finish_b(second_grad(queue, kept[k], fields[k], diffs[k])))

    last = projections - 1
    for k in ks:
        for s in range(1, side - late):
            accs[k] = early_one(k, accs[k], s)
        if k > 0:
            finish_one(k - 1)
            seconds[k - 1][0] = early_two(seconds[k - 1][0])
        sums.append(pieces_one(k, accs[k]))
        if k > 0:
            after = (lambda: finish_one(last)) if k == last else None
            fields.append(away_two(k - 1, *seconds[k - 1][0], after))
    if last == 0:
        finish_one(last)
    seconds[last][0] = early_two(seconds[last][0])
    fields.append(away_two(last, *seconds[last][0], None))
    kept = [kept_two(k, *seconds[k][0]) for k in reversed(ks)][::-1]
    for k in range(last):
        diff_two(k)
        grad_two(k)
    diff_two(last)
    new_a = jnp.stack(new_a, 1)
    queue.meta, new_a = lax.optimization_barrier((queue.meta, new_a))
    grad_two(last)
    return new_a, sum_rows(jnp.stack(values, 0))


def away_order(side):
    return (3, 1, 2) if side == 4 else tuple(range(1, side))


def solution(mesh):
    in_specs = (
        P(("layer", "row"), "col"),
        P(("layer", "col", "row"), None, None),
        P(("layer", "col", "row"), None, None),
        P("layer", ("row", "col"), None),
    )
    out_specs = (P(("layer", "col", "row"), None, None), P("layer", ("row", "col"), None))

    return jax.shard_map(
        per_device, mesh=mesh, in_specs=in_specs, out_specs=out_specs, check_vma=False
    )
```

```python
import jax
import jax.numpy as jnp
from jax import lax
from jax.experimental import pallas as pl
from jax.experimental.pallas import tpu as pltpu
from jax.sharding import PartitionSpec as P


CORES = 2
F32, BF16 = jnp.float32, jnp.bfloat16
VMEM_LIMIT = 12 * 2**20

SCALE_P = 2.0**-2
SCALE_G = 2.0**-7
SCALE_A = 2.0**-4
SCALE_F = 2.0**-17
SCALE_V = 2.0**-36


def encode(x, scale):
    u = x * scale
    return (u * jnp.abs(u) * (u * u)).astype(BF16)


def decode(code, scale):
    v = code.astype(F32)
    root = lax.rsqrt(lax.rsqrt(jnp.abs(v))) * (1.0 / scale)
    return jnp.where(v < 0, -root, root)


def encode_wide(x):
    u = x * SCALE_V
    return (u * jnp.abs(u)).astype(BF16)


def decode_wide(code):
    v = code.astype(F32)
    root = jnp.sqrt(jnp.abs(v)) * (1.0 / SCALE_V)
    return jnp.where(v < 0, -root, root)


def halves(x):
    high = x.astype(BF16)
    return high, (x - high.astype(F32)).astype(BF16)


def mm(a, b):
    return jnp.dot(a, b, preferred_element_type=F32)


class Queue:
    def __init__(self, meta):
        self.meta = meta

    def call(self, body, grid, ins, outs, shapes, args, scratch=(), alias=None, flops=0, limit=VMEM_LIMIT):
        moved = sum(a.size * a.dtype.itemsize for a in args)
        moved += sum(s.size * s.dtype.itemsize for s in shapes)
        spec = pltpu.PrefetchScalarGridSpec(
            num_scalar_prefetch=1,
            grid=grid,
            in_specs=ins,
            out_specs=outs,
            scratch_shapes=list(scratch),
        )
        got = pl.pallas_call(
            body,
            out_shape=shapes,
            grid_spec=spec,
            input_output_aliases=alias or {},
            cost_estimate=pl.CostEstimate(flops=flops, bytes_accessed=moved, transcendentals=0),
            compiler_params=pltpu.CompilerParams(
                dimension_semantics=("arbitrary",) * len(grid), vmem_limit_bytes=limit
            ),
        )(self.meta, *args)
        self.meta, *got = lax.optimization_barrier((self.meta, *got))
        return got[0] if len(got) == 1 else got


def shape(dims, dtype):
    return jax.ShapeDtypeStruct(dims, dtype)


def split_cov(queue, cov):
    rows, cols = cov.shape
    tile = min(rows, 256)

    def body(m, c, hi, lo):
        hi[...], lo[...] = halves(c[...])

    spec = pl.BlockSpec((tile, cols), lambda i, m: (i, 0))
    return queue.call(
        body, (rows // tile,), [spec], [spec, spec], [shape(cov.shape, BF16)] * 2, [cov],
    )


def place_b(queue, own, other, from_row, from_y, core_at):
    ys, side, projections, share, features = own.shape
    rank = ys * side * CORES * share

    def body(m, own, other, out):
        s = pl.program_id(0)
        for t in range(ys):
            place = (m[from_row + s] * ys + m[from_y + t]) * CORES
            for ref, core in ((own, m[core_at]), (other, 1 - m[core_at])):
                at = pl.ds(pl.multiple_of((place + core) * share, share), share)
                for k in range(projections):
                    out[k, at, :] = ref[t, 0, k]

    spec = pl.BlockSpec((ys, 1, projections, share, features), lambda s, m: (0, s, 0, 0, 0))
    return queue.call(
        body,
        (side,),
        [spec, spec],
        [pl.BlockSpec((projections, rank, features), lambda s, m: (0, 0, 0))],
        [shape((projections, rank, features), BF16)],
        [own, other],
    )


def project(queue, w, a, b, k):
    rank, features = b.shape[1:]
    n = w.shape[0]
    tile = min(n, 256)

    def body(m, w, a, b, code):
        diff = (w[...].astype(F32) - mm(a[...], b[0])).astype(BF16)
        proj = lax.dot_general(diff, b[0], (((1,), (1,)), ((), ())), preferred_element_type=F32)
        code[...] = encode(proj, SCALE_P)

    return queue.call(
        body,
        (n // tile,),
        [
            pl.BlockSpec((tile, features), lambda i, m: (i, k)),
            pl.BlockSpec((tile, rank), lambda i, m: (i, k)),
            pl.BlockSpec((1, rank, features), lambda i, m: (k, 0, 0)),
        ],
        [pl.BlockSpec((tile, rank), lambda i, m: (i, 0))],
        [shape((n, rank), BF16)],
        [w, a, b],
        flops=4 * n * rank * features,
    )


def product_one(queue, cov, blocks, acc, row_of, count, add=None, coded=False, ready=None, emit=False):
    hi, lo = cov
    n, width = blocks[0][0][0].shape
    fresh = ready is None
    whole = count * n == hi.shape[0]
    terms = len(blocks)
    tall = n
    if whole and count % 2 == 0:
        tall, count = 2 * n, count // 2

    def body(m, *refs):
        refs = list(refs)
        his, los, refs = refs[:terms], refs[terms : 2 * terms], refs[2 * terms :]
        if fresh:
            codes = [[refs.pop(0) for _ in got] for got, _ in blocks]
        else:
            p_hi, p_lo = refs.pop(0), refs.pop(0)
        acc_ref = refs.pop(0) if acc is not None else None
        add_ref = refs.pop(0) if add is not None else None
        out = refs.pop(0)
        if fresh:
            p_hi, p_lo = refs

        @pl.when(fresh and pl.program_id(0) == 0)
        def _():
            for t in range(terms):
                code = sum(ref[...].astype(F32) for ref in codes[t])
                p_hi[t], p_lo[t] = halves(decode(code, SCALE_P))

        got = None
        for t in range(terms):
            c = his[t][...]
            part = mm(c, p_hi[t]) + mm(c, p_lo[t]) + mm(los[t][...], p_hi[t])
            got = part if got is None else got + part
        if acc is not None:
            got = got + acc_ref[...]
        if add is not None:
            got = got + add_ref[...]
        out[...] = encode(got, SCALE_G) if coded else got

    specs = [
        pl.BlockSpec((tall, n), lambda i, m, at=at: (row_of(i, m), m[at])) for _, at in blocks
    ]
    codes = [code for got, _ in blocks for code in got] if fresh else list(ready)
    parts = pl.BlockSpec((terms, n, width), lambda i, m: (0, 0, 0))
    held = pl.BlockSpec((n, width), lambda i, m: (0, 0)) if fresh else parts
    ins = specs + specs + [held] * len(codes)
    args = [hi] * terms + [lo] * terms + codes
    alias = None
    if acc is not None:
        if whole:
            alias = {1 + len(args): 0}
        ins.append(pl.BlockSpec((tall, width), lambda i, m: (row_of(i, m), 0)))
        args.append(acc)
    if add is not None:
        ins.append(pl.BlockSpec((tall, width), lambda i, m: (i, 0)))
        args.append(add)
    return queue.call(
        body,
        (count,),
        ins,
        [pl.BlockSpec((tall, width), lambda i, m: (i, 0))] + [parts] * (2 * emit),
        [shape((count * tall, width), BF16 if coded else F32)]
        + [shape((terms, n, width), BF16)] * (2 * emit),
        args,
        scratch=[pltpu.VMEM((terms, n, width), BF16)] * (2 * (fresh and not emit)),
        alias=alias,
        flops=6 * terms * count * tall * n * width,
    )


def finish_grad(queue, part, codes, mirrored_a, step):
    n, width = part.shape
    tile = min(n, 128)
    count, pieces = len(codes), len(mirrored_a)

    def body(m, part, *rest):
        grad = part[...]
        for ref in rest[:count]:
            grad = grad + decode(ref[...], SCALE_G)
        grad_code, a_code = rest[count + pieces :]
        grad_code[...] = encode(grad, SCALE_G)
        a_new = step * grad
        for ref in rest[count : count + pieces]:
            a_new = a_new + ref[...].astype(F32)
        a_code[...] = encode(a_new.T, SCALE_A)

    spec = pl.BlockSpec((tile, width), lambda i, m: (i, 0))
    return queue.call(
        body,
        (n // tile,),
        [spec] * (1 + count + pieces),
        [spec, pl.BlockSpec((width, tile), lambda i, m: (0, i))],
        [shape((n, width), BF16), shape((width, n), BF16)],
        [part, *codes, *mirrored_a],
    )


def product_two(queue, cov, blocks, acc, col_of, count, coded=False, add=None, ready=None, emit=False):
    hi, lo = cov
    width, n = blocks[0][0].shape
    fresh = ready is None
    whole = count * n == hi.shape[1]
    terms = len(blocks)

    def body(m, *refs):
        refs = list(refs)
        his, los, refs = refs[:terms], refs[terms : 2 * terms], refs[2 * terms :]
        codes = [refs.pop(0) for _ in blocks] if fresh else []
        parts = None if fresh else refs.pop(0)
        acc_ref = refs.pop(0) if acc is not None else None
        add_ref = refs.pop(0) if add is not None else None
        out = refs.pop(0)
        if fresh:
            (parts,) = refs

        @pl.when(fresh and pl.program_id(0) == 0)
        def _():
            for t in range(terms):
                parts[t, :width], parts[t, width:] = halves(decode(codes[t][...], SCALE_A))

        got = None
        for t in range(terms):
            c = his[t][...]
            both = mm(parts[t], c)
            part = both[:width] + both[width:] + mm(parts[t, :width], los[t][...])
            got = part if got is None else got + part
        if acc is not None:
            got = got + acc_ref[...]
        if add is not None:
            got = got + decode(add_ref[...], SCALE_F)
        out[...] = encode(got, SCALE_F) if coded else got

    specs = [
        pl.BlockSpec((n, n), lambda i, m, row=row: (row(m), col_of(i, m))) for _, row in blocks
    ]
    whole_parts = pl.BlockSpec((terms, 2 * width, n), lambda i, m: (0, 0, 0))
    codes = [code for code, _ in blocks] if fresh else [ready]
    held = pl.BlockSpec((width, n), lambda i, m: (0, 0)) if fresh else whole_parts
    ins = specs + specs + [held] * len(codes)
    args = [hi] * terms + [lo] * terms + codes
    alias = None
    if acc is not None:
        if whole:
            alias = {1 + len(args): 0}
        ins.append(pl.BlockSpec((width, n), lambda i, m: (0, col_of(i, m))))
        args.append(acc)
    if add is not None:
        ins.append(pl.BlockSpec((width, n), lambda i, m: (0, i)))
        args.append(add)
    return queue.call(
        body,
        (count,),
        ins,
        [pl.BlockSpec((width, n), lambda i, m: (0, i))] + [whole_parts] * emit,
        [shape((width, count * n), BF16 if coded else F32)]
        + [shape((terms, 2 * width, n), BF16)] * emit,
        args,
        scratch=[pltpu.VMEM((terms, 2 * width, n), BF16)] * (fresh and not emit),
        alias=alias,
        flops=6 * terms * count * n * n * width,
    )


def second_diff(queue, grad_codes, w, a, b, k, step):
    n, rank = grad_codes[0].shape
    features = b.shape[2]
    tile = min(n, 256)
    pieces = len(grad_codes)

    def body(m, w, a, b, *rest):
        new_a, diff = rest[pieces:]
        code = rest[0][...].astype(F32)
        for ref in rest[1:pieces]:
            code = code + ref[...].astype(F32)
        a_new = a[...].astype(F32) + step * decode(code, SCALE_G)
        new_a[...] = a_new
        high, low = halves(a_new)
        value = mm(high, b[0]) + mm(low, b[0])
        diff[...] = (w[...].astype(F32) - value).astype(BF16)

    narrow = pl.BlockSpec((tile, rank), lambda i, m: (i, 0))
    return queue.call(
        body,
        (n // tile,),
        [
            pl.BlockSpec((tile, features), lambda i, m: (i, k)),
            pl.BlockSpec((tile, rank), lambda i, m: (i, k)),
            pl.BlockSpec((1, rank, features), lambda i, m: (k, 0, 0)),
        ]
        + [narrow] * pieces,
        [narrow, pl.BlockSpec((tile, features), lambda i, m: (i, 0))],
        [shape((n, rank), F32), shape((n, features), BF16)],
        [w, a, b, *grad_codes],
        flops=4 * n * rank * features,
    )


def second_grad(queue, own, codes, diff):
    rank, n = own.shape
    features = diff.shape[1]
    count = len(codes)
    tile = min(features, 512)

    def body(m, own, diff, *rest):
        out, f_hi, f_lo = rest[count:]

        @pl.when(pl.program_id(0) == 0)
        def _():
            field = own[...]
            for ref in rest[:count]:
                field = field + decode(ref[...], SCALE_F)
            f_hi[...], f_lo[...] = halves(field)

        out[...] = mm(f_hi[...], diff[...]) + mm(f_lo[...], diff[...])

    spec = pl.BlockSpec((rank, n), lambda i, m: (0, 0))
    return queue.call(
        body,
        (features // tile,),
        [spec, pl.BlockSpec((n, tile), lambda i, m: (0, i))] + [spec] * count,
        [pl.BlockSpec((rank, tile), lambda i, m: (0, i))],
        [shape((rank, features), F32)],
        [own, diff, *codes],
        scratch=[pltpu.VMEM((rank, n), BF16)] * 2,
        flops=4 * n * rank * features,
    )


def per_device(covariance, weight, factor_a, factor_b):
    side = lax.axis_size("row")
    ys = lax.axis_size("col") // CORES
    row = lax.axis_index("row")
    col = lax.axis_index("col")
    y, core = col // CORES, col % CORES
    n, projections, features = weight.shape
    rank = factor_a.shape[2]
    width = projections * rank
    share = factor_b.shape[1]
    step_a = 4.0 / features
    step_b = 8.0 / (n * side * side)

    def swap_core(x):
        return lax.ppermute(x, "col", [(i, i ^ 1) for i in range(ys * CORES)])

    def shift_y(x, s):
        pairs = [(i, (i // CORES + s) % ys * CORES + i % CORES) for i in range(ys * CORES)]
        return lax.ppermute(x, "col", pairs)

    def shift_row(x, s):
        return lax.ppermute(x, "row", [(i, i ^ s) for i in range(side)])

    def mirror(x):
        pairs = [(i * side + j, j * side + i) for i in range(side) for j in range(side)]
        return [lax.ppermute(x, ("row", "col"), pairs)]

    def pick(x, i, axis=0):
        return lax.dynamic_index_in_dim(x, i, axis, keepdims=False)

    hops, lanes = jnp.arange(side), jnp.arange(ys)
    meta = jnp.concatenate(
        [row ^ hops, row ^ hops, (y - lanes) % ys, (y + lanes) % ys, core[None]]
    ).astype(jnp.int32)
    from_row, to_row = 0, side
    from_y, to_y = 2 * side, 2 * side + ys
    core_at = 2 * side + 2 * ys
    here = [core, 1 - core, y, row]
    here += [(y + t) % ys for t in range(1, ys)] + [row ^ t for t in range(1, side)]
    here = [i.astype(jnp.uint32) for i in here]
    a = factor_a.reshape(n, width)
    w = weight.reshape(n, projections * features)
    meta, a, w, *here = lax.optimization_barrier((meta, a, w, *here))
    own_core, other_core, own_y, own_row = here[:4]
    next_y, next_row = here[3 : 3 + ys], here[2 + ys :]
    queue = Queue(meta)

    z = jnp.stack([factor_b] + [shift_row(factor_b, s) for s in range(1, side)])
    zy = jnp.stack([z] + [shift_y(z, s) for s in range(1, ys)])
    mirrored_a = [mirror(a[:, k * rank : (k + 1) * rank]) for k in range(projections)]
    zyc = swap_core(zy)
    if share % 16 == 0:
        b = place_b(queue, zy, zyc, from_row, from_y, core_at)
    else:
        both = jnp.where(core == 0, jnp.stack([zy, zyc]), jnp.stack([zyc, zy]))
        both = jnp.take(both, (y - lanes) % ys, axis=1)
        both = jnp.take(both, (row - hops) % side, axis=2)
        b = both.transpose(3, 2, 1, 0, 4, 5).reshape(projections, rank, features)

    ks = range(projections)
    relay = side == 4
    ends_in, ends_out, middle = [(0, 1), (3, 2)], [(1, 0), (2, 3)], [(1, 2), (2, 1)]

    def spread(code):
        got = [[code]] + [[shift_row(code, s)] for s in range(1, side)]
        if relay:
            got[3] = [lax.ppermute(code, "row", middle), lax.ppermute(got[2][0], "row", ends_out)]
        return got

    panels = []
    for k in ks:
        code = project(queue, w, a, b, k)
        panels.append(spread(code))
    cov = split_cov(queue, covariance)
    cov = [pltpu.with_memory_space_constraint(x, pltpu.VMEM) for x in cov]
    late = 2

    def early_one(k, acc, s):
        return product_one(queue, cov, [(panels[k][s], from_row + s)], acc, lambda i, m: i, side)

    def pieces_one(k, acc):
        blocks = [(panels[k][s], from_row + s) for s in range(side - late, side)]

        ready = None

        def piece(row_of, count, add=None, coded=False):
            first = ready is None
            return product_one(queue, cov, blocks, acc, row_of, count, add, coded, ready, first)

        far_other, *ready = piece(lambda i, m: m[to_y + 1 + i] * CORES + 1 - m[core_at], ys - 1)
        far_add = swap_core(far_other)
        near_other = piece(lambda i, m: m[to_y] * CORES + 1 - m[core_at], 1)
        near_add = swap_core(near_other)
        far_code = piece(
            lambda i, m: m[to_y + 1 + i] * CORES + m[core_at], ys - 1, add=far_add, coded=True
        )
        far = [shift_y(far_code[(s - 1) * n : s * n], s) for s in range(1, ys)]
        near = piece(lambda i, m: m[to_y] * CORES + m[core_at], 1, add=near_add)
        return near, far

    def start_two(k, near, far):
        grad_code, a_code = finish_grad(queue, near, far, mirrored_a[k], step_a)
        codes = [a_code] + [shift_y(a_code, s) for s in range(1, ys)]
        others = [swap_core(x) for x in codes]
        blocks = []
        for s in range(ys):
            blocks.append((codes[s], lambda m, s=s: m[from_y + s] * CORES + m[core_at]))
            blocks.append((others[s], lambda m, s=s: m[from_y + s] * CORES + 1 - m[core_at]))
        return blocks, mirror(grad_code)

    def early_two(blocks):
        acc = None
        for block in blocks[:-late]:
            acc = product_two(queue, cov, [block], acc, lambda i, m: i, side)
        return acc, blocks[-late:]

    def away_two(k, acc, blocks, between):
        landed, passed, ready = [], None, None
        for hop in away_order(side):
            piece = product_two(
                queue,
                cov,
                blocks,
                acc,
                lambda i, m, hop=hop: m[to_row + hop],
                1,
                coded=True,
                add=passed if relay and hop == 2 else None,
                ready=ready,
                emit=ready is None,
            )
            if ready is None:
                piece, ready = piece
            parts_two[k] = ready
            if relay and hop == 3:
                passed = lax.ppermute(piece, "row", ends_in)
                landed.append(lax.ppermute(piece, "row", middle))
            else:
                landed.append(shift_row(piece, hop))
            if between is not None:
                between()
                between = None
        return landed

    def kept_two(k, acc, blocks):
        return product_two(
            queue, cov, blocks, acc, lambda i, m: m[to_row], 1,
            ready=parts_two[k],
        )

    def finish_b(value):
        value = value.reshape(side, ys, CORES, share, features)
        value = pick(value, own_core, 2) + swap_core(pick(value, other_core, 2))
        mine = pick(value, own_y, 1)
        for s in range(1, ys):
            away = encode_wide(pick(value, next_y[s], 1))
            mine = mine + decode_wide(shift_y(away, s))
        return mine

    def sum_rows(mine):
        total = pick(mine, own_row, 1)
        for s in range(1, side):
            away = encode_wide(pick(mine, next_row[s], 1))
            total = total + decode_wide(shift_row(away, s))
        return factor_b.astype(F32) + step_b * total

    accs = [early_one(k, None, 0) for k in ks]
    sums, seconds, fields, values = [], [], [], []

    new_a, diffs, parts_two = [], [], {}

    def finish_one(k):
        blocks, back = start_two(k, *sums[k])
        seconds.append([blocks, back])

    def diff_two(k):
        a_new, diff = second_diff(queue, seconds[k][1], w, a, b, k, step_a)
        new_a.append(a_new)
        diffs.append(diff)

    def grad_two(k):
        values.append(finish_b(second_grad(queue, kept[k], fields[k], diffs[k])))

    last = projections - 1
    for k in ks:
        for s in range(1, side - late):
            accs[k] = early_one(k, accs[k], s)
        if k > 0:
            finish_one(k - 1)
            seconds[k - 1][0] = early_two(seconds[k - 1][0])
        sums.append(pieces_one(k, accs[k]))
        if k > 0:
            after = (lambda: finish_one(last)) if k == last else None
            fields.append(away_two(k - 1, *seconds[k - 1][0], after))
    if last == 0:
        finish_one(last)
    seconds[last][0] = early_two(seconds[last][0])
    fields.append(away_two(last, *seconds[last][0], None))
    kept = [kept_two(k, *seconds[k][0]) for k in reversed(ks)][::-1]
    for k in range(last):
        diff_two(k)
        grad_two(k)
    diff_two(last)
    new_a = jnp.stack(new_a, 1)
    queue.meta, new_a = lax.optimization_barrier((queue.meta, new_a))
    grad_two(last)
    return new_a, sum_rows(jnp.stack(values, 0))


def away_order(side):
    return (3, 1, 2) if side == 4 else tuple(range(1, side))


def solution(mesh):
    in_specs = (
        P(("layer", "row"), "col"),
        P(("layer", "col", "row"), None, None),
        P(("layer", "col", "row"), None, None),
        P("layer", ("row", "col"), None),
    )
    out_specs = (P(("layer", "col", "row"), None, None), P("layer", ("row", "col"), None))

    return jax.shard_map(
        per_device, mesh=mesh, in_specs=in_specs, out_specs=out_specs, check_vma=False
    )
```
